256 devices in a mesh: leaf: 256 (over x, z, y, core).
Axes of the slice: x: 4, y: 4, z: 8, core: 2. Of those that a mesh axis runs over, the one named last changes fastest.
Arguments:
- near_blocks: bfloat16 [512, 26, 256, 256], P('leaf'), may hold values from -0.0582 to 0.0582
- diag_blocks: bfloat16 [512, 256, 256], P('leaf'), as said below
- bases: bfloat16 [512, 256, 256], P('leaf'), as said below
- leaf_nbrs: int32 [512, 26], P('leaf'), may hold values from -1 to 511, as said below
- parent_nbrs: int32 [64, 5], replicated, may hold values from 0 to 63, as said below
Outputs:
- leaf_factor: float32 [512, 128, 128], P('leaf')
- leaf_panel: float32 [512, 128, 128], P('leaf')
- merged: float32 [512, 5, 128, 1024], P('leaf')
- parent_block: float32 [65536, 1024], P('leaf')
The draws below stay inside these ranges and needn't reach their ends.
Inputs may be any that keep to these rules, and one draw needn't show every extreme that they name: `leaf_nbrs`: row i lists distinct leaves j with j != i and |j - i| <= 16; live entries come first and -1 fills the rest; every row has at least 13 live entries and some row has all 26. `parent_nbrs`: row P begins with P itself, followed by the other 4 parents nearest to P in numbering, distinct, equally near ones in any order. `diag_blocks`: each block is symmetric positive definite. `bases`: each basis is an orthogonal matrix rounded to bfloat16.
All inputs are finite; a program needn't handle non-finite values.
Results may differ from the reference program's by a relative error of at most 0.001.
The reference program's roundings to bfloat16 on the way count: a program that leaves them out, or rounds other values in their place, can miss the bound.
Values may be sent and summed in bfloat16 or wider, within the bound.
No kernel may reach another device: no remote copies, remote signals or barrier semaphores. Data moves between devices by JAX's collectives and lax.ppermute only.
A program may use at most 128 MiB of HBM per device.

```python
import jax
import jax.numpy as jnp
from jax import lax

LR = 256
RANK = 128
NB = 26
REACH = 16
CHILDREN = 8
LEAVES = 512
PARENTS = 64
PNB = 5


def draw_near_blocks(key, part):
    base_key = jax.random.fold_in(key, 53)

    def one_leaf(leaf_index):
        leaf_key = jax.random.fold_in(base_key, leaf_index)
        values = jnp.clip(0.013 * jax.random.normal(leaf_key, (NB, LR, LR), jnp.float32), -0.058, 0.058)
        return values.astype(jnp.bfloat16)
    return lax.map(one_leaf, jnp.arange(LEAVES, dtype=jnp.int32))


def draw_diag_blocks(key, part):
    key_scale, key_mix = jax.random.split(jax.random.fold_in(key, 11))
    scales = jnp.exp(jax.random.uniform(key_scale, (LEAVES, LR), jnp.float32, jnp.log(1.0), jnp.log(4.0)))

    def one_leaf(leaf_index):
        leaf_key = jax.random.fold_in(key_mix, leaf_index)
        mixing = jax.random.normal(leaf_key, (LR, LR), jnp.float32)
        gram = jnp.dot(mixing, mixing.T, precision=lax.Precision.HIGHEST) / LR
        return 0.5 * (gram + gram.T)
    grams = lax.map(one_leaf, jnp.arange(LEAVES, dtype=jnp.int32))
    blocks = grams + scales[:, :, None] * jnp.eye(LR, dtype=jnp.float32)[None]
    return blocks.astype(jnp.bfloat16)


def draw_bases(key, part):
    source = jax.random.normal(jax.random.fold_in(key, 23), (LEAVES, LR, LR), jnp.float32)
    orthogonal, upper_part = jnp.linalg.qr(source)
    return orthogonal.astype(jnp.bfloat16)


def draw_leaf_nbrs(key, part):
    base_key = jax.random.fold_in(key, 37)
    key_rank, key_count, key_full = jax.random.split(base_key, 3)
    offsets = jnp.concatenate([jnp.arange(-REACH, 0), jnp.arange(1, REACH + 1)]).astype(jnp.int32)
    row_keys = jax.random.split(key_rank, LEAVES)
    row_ranks = jax.vmap(lambda row_key: jax.random.permutation(row_key, 2 * REACH))(row_keys).astype(jnp.int32)
    leaves = jnp.arange(LEAVES, dtype=jnp.int32)
    targets = leaves[:, None] + offsets[None, :]
    in_range = (targets >= 0) & (targets < LEAVES)
    scores = in_range.astype(jnp.int32) * 1024 + row_ranks
    top_scores, picked_slots = lax.top_k(scores, NB)
    chosen = leaves[:, None] + offsets[picked_slots]
    counts = jax.random.randint(key_count, (LEAVES,), 13, NB + 1)
    full_leaf = jax.random.randint(key_full, (), REACH, LEAVES - REACH)
    counts = jnp.where(leaves == full_leaf, NB, counts)
    slot_ids = jnp.arange(NB, dtype=jnp.int32)[None, :]
    is_live = (slot_ids < counts[:, None]) & (top_scores >= 1024)
    return jnp.where(is_live, chosen, -1).astype(jnp.int32)


def draw_parent_nbrs(key, part):
    row_ranks = jax.random.permutation(jax.random.fold_in(key, 41), PARENTS).astype(jnp.int32)
    parents = jnp.arange(PARENTS, dtype=jnp.int32)
    distance = jnp.abs(parents[:, None] - parents[None, :])
    scores = -distance * 4096 + row_ranks[None, :]
    top_scores, picked = lax.top_k(scores, PNB)
    return picked.astype(jnp.int32)


def setup_inputs(seed: int = 0) -> dict:
    key_of = jax.random.split(jax.random.key(seed), 6)
    near_blocks = draw_near_blocks(jax.random.fold_in(key_of[5], 71), 0)
    diag_blocks = draw_diag_blocks(jax.random.fold_in(key_of[5], 71), 0)
    bases = draw_bases(jax.random.fold_in(key_of[5], 71), 0)
    leaf_nbrs = draw_leaf_nbrs(jax.random.fold_in(key_of[5], 71), 0)
    parent_nbrs = draw_parent_nbrs(jax.random.fold_in(key_of[5], 71), 0)
    return dict(near_blocks=near_blocks, diag_blocks=diag_blocks, bases=bases, leaf_nbrs=leaf_nbrs, parent_nbrs=parent_nbrs)


highest = lax.Precision.HIGHEST

def lower_solve(lower_factor, right_side):
    return lax.linalg.triangular_solve(lower_factor, right_side, left_side=True, lower=True)

def back_solve(lower_factor, right_side):
    return lax.linalg.triangular_solve(lower_factor, right_side, left_side=True, lower=True, transpose_a=True)

def factor_leaf(block, basis):
    basis_wide = basis.astype(jnp.float32)
    half_proj = jnp.dot(basis_wide.T, block.astype(jnp.float32), precision=highest).astype(jnp.bfloat16)
    half_proj = lax.optimization_barrier(half_proj).astype(jnp.float32)
    dense = jnp.dot(half_proj, basis_wide, precision=highest)
    redundant = LR - RANK
    lower_factor = jnp.linalg.cholesky(dense[:redundant, :redundant])
    panel_rows = lower_solve(lower_factor, dense[:redundant, redundant:])
    skeleton = dense[redundant:, redundant:] - jnp.dot(panel_rows.T, panel_rows, precision=highest)
    shift_rows = back_solve(lower_factor, panel_rows)
    return (lower_factor, panel_rows, skeleton, shift_rows)

def reference(near_blocks, diag_blocks, bases, leaf_nbrs, parent_nbrs):
    redundant = LR - RANK
    leaf_factor, leaf_panel, skeleton, shift_wide = jax.vmap(factor_leaf)(diag_blocks, bases)
    leaf_shift = lax.optimization_barrier(shift_wide.astype(jnp.bfloat16)).astype(jnp.float32)

    def leaf_row(leaf_index):
        neighbours = leaf_nbrs[leaf_index]
        is_live = neighbours >= 0
        clipped = jnp.maximum(neighbours, 0)
        basis_wide = bases[leaf_index].astype(jnp.float32)
        half_proj = jnp.einsum('ba,nbc->nac', basis_wide, near_blocks[leaf_index].astype(jnp.float32), precision=highest).astype(jnp.bfloat16)
        half_proj = lax.optimization_barrier(half_proj).astype(jnp.float32)
        coupled = jnp.einsum('nac,ncb->nab', half_proj, bases[clipped].astype(jnp.float32), precision=highest)
        own_shift = leaf_shift[leaf_index]
        first_term = jnp.einsum('ka,nkb->nab', own_shift, coupled[:, :redundant, redundant:], precision=highest)
        second_term = jnp.einsum('nak,nkb->nab', coupled[:, redundant:, :redundant], leaf_shift[clipped], precision=highest)
        near_schur = jnp.where(is_live[:, None, None], coupled[:, redundant:, redundant:] - first_term - second_term, jnp.float32(0.0))
        parent = leaf_index // CHILDREN
        position = leaf_index % CHILDREN
        targets = parent_nbrs[parent]
        children = jnp.arange(CHILDREN, dtype=jnp.int32)
        slot_hits = is_live[None, None, :] & (clipped[None, None, :] // CHILDREN == targets[:, None, None]) & (clipped[None, None, :] % CHILDREN == children[None, :, None])
        self_hit = (targets[:, None] == parent) & (children[None, :] == position)
        parent_rows = jnp.einsum('qbn,nxy->qxby', slot_hits.astype(jnp.float32), near_schur, precision=highest)
        parent_rows = parent_rows + self_hit.astype(jnp.float32)[:, None, :, None] * skeleton[leaf_index][None, :, None, :]
        parent_rows = parent_rows.reshape(PNB, RANK, CHILDREN * RANK)
        return (parent_rows, parent_rows[0])
    merged, diagonal_rows = lax.map(leaf_row, jnp.arange(LEAVES, dtype=jnp.int32))
    blocks = diagonal_rows.reshape(PARENTS, CHILDREN * RANK, CHILDREN * RANK)
    symmetric = 0.5 * (blocks + jnp.transpose(blocks, (0, 2, 1)))
    return (leaf_factor, leaf_panel, merged, symmetric.reshape(LEAVES * RANK, CHILDREN * RANK))
```

```python
import jax
import jax.numpy as jnp
from jax import lax
from jax.experimental import pallas as pl
from jax.experimental.pallas import tpu as pltpu
from jax.sharding import PartitionSpec as P

RANK = 128
REACH = 16
CHILDREN = 8
SLOTS = 26
PNB = 5
REACH_CHIPS = 4
WINDOW = 36
VMEM = 48 * 1024 * 1024


F32 = jnp.float32
BF = jnp.bfloat16

def split(x):
    hi = x.astype(BF)
    lo = (x - hi.astype(F32)).astype(BF)
    return hi, lo

def dot00(a, b):
    return lax.dot_general(a, b, (((0,), (0,)), ((), ())), preferred_element_type=F32)

def dot00_3(a, b):
    ah, al = split(a); bh, bl = split(b)
    return dot00(jnp.concatenate([ah, ah, al], 0), jnp.concatenate([bh, bl, bh], 0))

def bc(x):
    return jnp.broadcast_to(x, (8, 128))

def eliminate(blocks, out):
    sub = lax.broadcasted_iota(jnp.int32, (8, 128), 0)
    count = len(blocks)
    done = []
    for k in range(count):
        yield
        parts = blocks[k]
        left = parts[0]
        cols = [bc(left[:, 8*k+j:8*k+j+1]) for j in range(8)]
        s = [[bc(cols[j][i:i+1, :]) for j in range(i+1)] for i in range(8)]
        r = [None]*8
        L = [[None]*8 for _ in range(8)]
        for j in range(8):
            r[j] = lax.rsqrt(s[j][j])
            for i in range(j+1, 8):
                L[i][j] = s[i][j]*r[j]
            for i in range(j+1, 8):
                for m in range(j+1, i+1):
                    s[i][m] = s[i][m] - L[i][j]*L[m][j]
        rows = []
        for j in range(8):
            row = []
            for q, part in enumerate(parts):
                x = bc(part[j:j+1, :])
                for m in range(j):
                    x = x - L[j][m]*rows[m][q]
                row.append(x*r[j])
            rows.append(row)
        packed = []
        for q in range(len(parts)):
            x = rows[0][q]
            for j in range(1, 8):
                x = jnp.where(sub == j, rows[j][q], x)
            packed.append(x)
        done.append(packed)
        if k + 1 < count:
            nxt = blocks[k+1]
            cb = [bc(nxt[0][:, 8*k+j:8*k+j+1]) for j in range(8)]
            lc = []
            new = list(nxt)
            for j in range(8):
                x = cb[j]
                for m in range(j):
                    x = x - lc[m]*L[j][m]
                x = x*r[j]
                lc.append(x)
                new = [new[q] - x*rows[j][q] for q in range(len(new))]
            blocks[k+1] = new
        if k + 2 < count:
            wide = jnp.concatenate(packed, 1)
            upd = dot00_3(packed[0], wide)
            for ib in range(k+2, count):
                blocks[ib] = [blocks[ib][q] - upd[8*ib:8*ib+8, 128*q:128*q+128] for q in range(len(packed))]
    out.extend(done)

def k0_body(u_ref, a_ref, f_ref, p_ref, sk_ref, s_ref, d_ref):
    row = lax.broadcasted_iota(jnp.int32, (128, 128), 0)
    col = lax.broadcasted_iota(jnp.int32, (128, 128), 1)
    eye = jnp.where(row == col, 1.0, 0.0).astype(F32)
    outs = []; gens = []
    prep = []
    for l in range(2):
        u = u_ref[l]
        half = dot00(u, a_ref[l]).astype(BF)
        dense = jnp.dot(half, u, preferred_element_type=F32)
        arr = dense[:128, :128]
        arr = 0.5*(arr + arr.T)
        prep.append((u, dense, arr))
    for l in range(2):
        u, dense, arr = prep[l]
        rs = dense[:128, 128:]
        blocks = [[arr[8*i:8*i+8], rs[8*i:8*i+8], eye[8*i:8*i+8]] for i in range(16)]
        outs.append([])
        gens.append(eliminate(blocks, outs[-1]))
    for _ in range(17):
        for g in gens:
            next(g, None)
    for l in range(2):
        u, dense, arr = prep[l]
        done = outs[l]
        upper = jnp.concatenate([d[0] for d in done], 0)
        upper = jnp.where(row <= col, upper, 0.0)
        panel = jnp.concatenate([d[1] for d in done], 0)
        inv = jnp.concatenate([d[2] for d in done], 0)
        f_ref[l] = upper.T
        p_ref[l] = panel
        shift = dot00_3(inv, panel).astype(BF)
        s_ref[l] = shift
        d_ref[l] = jnp.dot(u[:, :128], shift, preferred_element_type=F32).astype(BF)
        sk_ref[l] = dense[128:, 128:] - dot00_3(panel, panel)

def k0(bases, diag):
    sd = jax.ShapeDtypeStruct
    return pl.pallas_call(
        k0_body,
        out_shape=(sd((2,128,128),F32), sd((2,128,128),F32), sd((2,128,128),F32), sd((2,128,128),BF), sd((2,256,128),BF)),
        compiler_params=pltpu.CompilerParams(vmem_limit_bytes=48*1024*1024),
        name="leaf_elimination",
    )(bases, diag)


def window_copies(pieces, win, sems, core):
    own, other = pieces[0], pieces[1]
    copies = []

    def put(src, base, size):
        dst = win.at[pl.ds(base, size)]
        copies.append(pltpu.make_async_copy(src, dst, sems.at[len(copies)]))

    put(own, 16 + 2 * core, 2)
    put(other, 18 - 2 * core, 2)
    for k in range(1, REACH_CHIPS + 1):
        near, far = pieces[2 * k], pieces[2 * k + 1]
        low, high = 4 * (4 - k), 4 * (4 + k)
        put(near, jnp.where(core == 0, low, high), 4)
        put(far, jnp.where(core == 0, high, low), 4)
    return copies


def window_slot(leaf, device):
    pair = device // 2
    below = leaf // 4 < pair
    turned = jnp.where(below, leaf ^ 2, leaf)
    return turned - 4 * pair + REACH


def near_body(nbrs, u_ref, s_ref, a_ref, *refs):
    pieces = refs[:10]
    p1_ref, hs_ref, ut_ref, st_ref, win, sems = refs[10:]
    device = lax.axis_index("leaf")
    leaf, part = pl.program_id(0), pl.program_id(1)
    core = device % 2

    @pl.when((leaf == 0) & (part == 0))
    def _():
        copies = window_copies(pieces, win, sems, core)
        for c in copies:
            c.start()
        for c in copies:
            c.wait()

    @pl.when(part == 0)
    def _():
        ut_ref[...] = u_ref[0].T
        st_ref[...] = s_ref[0].T

    ut = ut_ref[...]
    st = st_ref[...]
    own = 2 * device + leaf
    count = a_ref.shape[1]
    for n in range(count):
        j = nbrs[leaf, part * count + n]
        j = jnp.where(j < 0, own, j)
        half = jnp.dot(ut, a_ref[0, n], preferred_element_type=F32).astype(BF)
        top, bottom = half[:RANK], half[RANK:]
        grown = bottom.astype(F32) - jnp.dot(st, top, preferred_element_type=F32)
        gh, gl = split(grown)
        us = win[window_slot(j, device)]
        both = jnp.dot(jnp.concatenate([gh, gl], 0), us, preferred_element_type=F32)
        p1_ref[0, n] = both[:RANK] + both[RANK:]
        hs_ref[0, n] = bottom


def near_products(leaf_nbrs, bases, shift, near_blocks, pieces):
    sd = jax.ShapeDtypeStruct
    parts = 2
    count = SLOTS // parts
    hbm = pl.BlockSpec(memory_space=pl.ANY)
    return pl.pallas_call(
        near_body,
        grid_spec=pltpu.PrefetchScalarGridSpec(
            num_scalar_prefetch=1,
            grid=(2, parts),
            in_specs=[
                pl.BlockSpec((1, 256, 256), lambda l, p, nb: (l, 0, 0)),
                pl.BlockSpec((1, RANK, RANK), lambda l, p, nb: (l, 0, 0)),
                pl.BlockSpec((1, count, 256, 256), lambda l, p, nb: (l, p, 0, 0)),
            ]
            + [hbm] * 10,
            out_specs=[
                pl.BlockSpec((1, count, RANK, RANK), lambda l, p, nb: (l, p, 0, 0)),
                pl.BlockSpec((1, count, RANK, 256), lambda l, p, nb: (l, p, 0, 0)),
            ],
            scratch_shapes=[
                pltpu.VMEM((256, 256), BF),
                pltpu.VMEM((RANK, RANK), BF),
                pltpu.VMEM((WINDOW, 256, RANK), BF),
                pltpu.SemaphoreType.DMA((10,)),
            ],
        ),
        out_shape=(sd((2, SLOTS, RANK, RANK), F32), sd((2, SLOTS, RANK, 256), BF)),
        compiler_params=pltpu.CompilerParams(vmem_limit_bytes=VMEM),
        name="near_products",
    )(leaf_nbrs, bases, shift, near_blocks, *pieces)


def merge_body(nbrs, pnbrs, p1_ref, hs_ref, sk_ref, *refs):
    pieces = refs[:10]
    out_ref, ex_ref, win, sems = refs[10:]
    device = lax.axis_index("leaf")
    leaf = pl.program_id(0)
    core = device % 2

    @pl.when(leaf == 0)
    def _():
        copies = window_copies(pieces, win, sems, core)
        for c in copies:
            c.start()
        for c in copies:
            c.wait()

    own = 2 * device + leaf
    parent = own // CHILDREN
    out_ref[...] = jnp.zeros_like(out_ref)
    mine = pl.multiple_of((own % CHILDREN) * RANK, RANK)
    for q in range(PNB):

        @pl.when(pnbrs[parent, q] == parent)
        def _():
            out_ref[0, q, :, pl.ds(mine, RANK)] = sk_ref[0]

    for n in range(SLOTS):
        j = nbrs[leaf, n]
        goal = jnp.maximum(j, 0) // CHILDREN
        q = jnp.int32(-1)
        for t in range(PNB):
            q = jnp.where(pnbrs[parent, t] == goal, t, q)

        @pl.when((j >= 0) & (q >= 0))
        def _():
            at = pl.multiple_of((j % CHILDREN) * RANK, RANK)
            d = win[window_slot(j, device)]
            out_ref[0, q, :, pl.ds(at, RANK)] = p1_ref[0, n] - jnp.dot(
                hs_ref[0, n], d, preferred_element_type=F32
            )

    place = device % 4
    for m in range(1, 4):
        at = pl.multiple_of((place ^ m) * 256, 256)
        ex_ref[m - 1] = out_ref[0, 0, :, pl.ds(at, 256)].T.astype(BF)


def merge(leaf_nbrs, parent_nbrs, p1, hs, skeleton, pieces):
    sd = jax.ShapeDtypeStruct
    hbm = pl.BlockSpec(memory_space=pl.ANY)
    return pl.pallas_call(
        merge_body,
        grid_spec=pltpu.PrefetchScalarGridSpec(
            num_scalar_prefetch=2,
            grid=(2,),
            in_specs=[
                pl.BlockSpec((1, SLOTS, RANK, RANK), lambda l, a, b: (l, 0, 0, 0)),
                pl.BlockSpec((1, SLOTS, RANK, 256), lambda l, a, b: (l, 0, 0, 0)),
                pl.BlockSpec((1, RANK, RANK), lambda l, a, b: (l, 0, 0)),
            ]
            + [hbm] * 10,
            out_specs=[
                pl.BlockSpec((1, PNB, RANK, CHILDREN * RANK), lambda l, a, b: (l, 0, 0, 0)),
                pl.BlockSpec((3, 256, RANK), lambda l, a, b: (0, 0, l)),
            ],
            scratch_shapes=[
                pltpu.VMEM((WINDOW, 256, RANK), BF),
                pltpu.SemaphoreType.DMA((10,)),
            ],
        ),
        out_shape=(sd((2, PNB, RANK, CHILDREN * RANK), F32), sd((3, 256, 256), BF)),
        compiler_params=pltpu.CompilerParams(vmem_limit_bytes=VMEM),
        name="merge_rows",
    )(leaf_nbrs, parent_nbrs, p1, hs, skeleton, *pieces)


def symmetric_body(rows_ref, r1_ref, r2_ref, r3_ref, out_ref):
    place = lax.axis_index("leaf") % 4
    rows = [rows_ref[0, 0], rows_ref[1, 0]]
    del rows
    for m, ref in enumerate((None, r1_ref, r2_ref, r3_ref)):
        at = pl.multiple_of((place ^ m) * 256, 256)
        own = jnp.concatenate([rows_ref[l, 0, :, pl.ds(at, 256)] for l in range(2)], 0)
        turned = own.T if m == 0 else ref[...].astype(F32)
        out_ref[:, pl.ds(at, 256)] = 0.5 * (own + turned)


def symmetric(merged, received):
    return pl.pallas_call(
        symmetric_body,
        grid=(1,),
        in_specs=[pl.BlockSpec((2, 1, RANK, CHILDREN * RANK), lambda i: (0, 0, 0, 0))]
        + [pl.BlockSpec((256, 256), lambda i: (0, 0))] * 3,
        out_specs=pl.BlockSpec((256, CHILDREN * RANK), lambda i: (0, 0)),
        out_shape=jax.ShapeDtypeStruct((256, CHILDREN * RANK), F32),
        compiler_params=pltpu.CompilerParams(vmem_limit_bytes=VMEM),
        name="symmetric_rows",
    )(merged, *received)


def swap(value, mask):
    pairs = [(source, source ^ mask) for source in range(lax.axis_size("leaf"))]
    return lax.ppermute(value, "leaf", pairs)


def across(value, apart):
    count = lax.axis_size("leaf")
    pairs = []
    for lower in range(1, count, 2):
        upper = (lower - 1 + 2 * apart) % count
        pairs += [(lower, upper), (upper, lower)]
    return lax.ppermute(value, "leaf", pairs)


def spread(own):
    other = swap(own, 1)
    both = jnp.concatenate([own, other])
    first = across(both, 1)
    third = across(both, 3)
    fourth = across(both, 4)
    first_other = swap(first, 1)
    second = across(first_other, 1)
    return (
        own, other, first, first_other, second, swap(second, 1),
        third, swap(third, 1), fourth, swap(fourth, 1),
    )


def local(near_blocks, diag_blocks, bases, leaf_nbrs, parent_nbrs):
    skeleton_bases = spread(bases[:, :, RANK:])
    leaf_factor, leaf_panel, skeleton, leaf_shift, turned = k0(bases, diag_blocks)
    turned_bases = spread(turned)
    p1, hs = near_products(leaf_nbrs, bases, leaf_shift, near_blocks, skeleton_bases)
    merged, exchange = merge(leaf_nbrs, parent_nbrs, p1, hs, skeleton, turned_bases)
    received = [swap(exchange[m - 1], m) for m in range(1, 4)]
    parent_block = symmetric(merged, received)
    return (leaf_factor, leaf_panel, merged, parent_block)


def solution(mesh):
    in_specs = (
        P("leaf", None, None, None),
        P("leaf", None, None),
        P("leaf", None, None),
        P("leaf", None),
        P(),
    )
    out_specs = (
        P("leaf", None, None),
        P("leaf", None, None),
        P("leaf", None, None, None),
        P("leaf", None),
    )
    return jax.shard_map(local, mesh=mesh, in_specs=in_specs, out_specs=out_specs, check_vma=False)
```

```python
import jax
import jax.numpy as jnp
from jax import lax
from jax.experimental import pallas as pl
from jax.experimental.pallas import tpu as pltpu
from jax.sharding import PartitionSpec as P

RANK = 128
REACH = 16
CHILDREN = 8
SLOTS = 26
PNB = 5
REACH_CHIPS = 4
WINDOW = 36
GROUP = 6 + 7
RATE = 1.1e15
VMEM = 24 * 1024 * 1024


F32 = jnp.float32
BF = jnp.bfloat16

def split(x):
    hi = x.astype(BF)
    lo = (x - hi.astype(F32)).astype(BF)
    return hi, lo

def dot00(a, b):
    return lax.dot_general(a, b, (((0,), (0,)), ((), ())), preferred_element_type=F32)

def dot00_3(a, b):
    ah, al = split(a); bh, bl = split(b)
    return dot00(jnp.concatenate([ah, ah, al], 0), jnp.concatenate([bh, bl, bh], 0))

def bc(x):
    return jnp.broadcast_to(x, (8, 128))

def eliminate(blocks, out):
    sub = lax.broadcasted_iota(jnp.int32, (8, 128), 0)
    count = len(blocks)
    done = []
    for k in range(count):
        yield
        parts = blocks[k]
        left = parts[0]
        cols = [bc(left[:, 8*k+j:8*k+j+1]) for j in range(8)]
        s = [[bc(cols[j][i:i+1, :]) for j in range(i+1)] for i in range(8)]
        r = [None]*8
        L = [[None]*8 for _ in range(8)]
        for j in range(8):
            r[j] = lax.rsqrt(s[j][j])
            for i in range(j+1, 8):
                L[i][j] = s[i][j]*r[j]
            for i in range(j+1, 8):
                for m in range(j+1, i+1):
                    s[i][m] = s[i][m] - L[i][j]*L[m][j]
        rows = []
        for j in range(8):
            row = []
            for q, part in enumerate(parts):
                x = bc(part[j:j+1, :])
                for m in range(j):
                    x = x - L[j][m]*rows[m][q]
                row.append(x*r[j])
            rows.append(row)
        packed = []
        for q in range(len(parts)):
            x = rows[0][q]
            for j in range(1, 8):
                x = jnp.where(sub == j, rows[j][q], x)
            packed.append(x)
        done.append(packed)
        if k + 1 < count:
            nxt = blocks[k+1]
            cb = [bc(nxt[0][:, 8*k+j:8*k+j+1]) for j in range(8)]
            lc = []
            new = list(nxt)
            for j in range(8):
                x = cb[j]
                for m in range(j):
                    x = x - lc[m]*L[j][m]
                x = x*r[j]
                lc.append(x)
                new = [new[q] - x*rows[j][q] for q in range(len(new))]
            blocks[k+1] = new
        if k + 2 < count:
            wide = jnp.concatenate(packed, 1)
            upd = dot00_3(packed[0], wide)
            for ib in range(k+2, count):
                blocks[ib] = [blocks[ib][q] - upd[8*ib:8*ib+8, 128*q:128*q+128] for q in range(len(packed))]
    out.extend(done)

def cost(microseconds):
    return pl.CostEstimate(flops=int(microseconds * 1e-6 * RATE), bytes_accessed=0, transcendentals=0)


def k0_body(u_hbm, a_hbm, f_ref, p_ref, sk_ref, s_ref, d_ref, u_ref, a_ref, sems):
    loads = [
        pltpu.make_async_copy(u_hbm, u_ref, sems.at[0]),
        pltpu.make_async_copy(a_hbm, a_ref, sems.at[1]),
    ]
    for load in loads:
        load.start()
    for load in loads:
        load.wait()
    row = lax.broadcasted_iota(jnp.int32, (128, 128), 0)
    col = lax.broadcasted_iota(jnp.int32, (128, 128), 1)
    eye = jnp.where(row == col, 1.0, 0.0).astype(F32)
    outs = []; gens = []
    prep = []
    for l in range(2):
        u = u_ref[l]
        half = dot00(u, a_ref[l]).astype(BF)
        dense = jnp.dot(half, u, preferred_element_type=F32)
        arr = dense[:128, :128]
        arr = 0.5*(arr + arr.T)
        prep.append((u, dense, arr))
    for l in range(2):
        u, dense, arr = prep[l]
        rs = dense[:128, 128:]
        blocks = [[arr[8*i:8*i+8], rs[8*i:8*i+8], eye[8*i:8*i+8]] for i in range(16)]
        outs.append([])
        gens.append(eliminate(blocks, outs[-1]))
    for _ in range(17):
        for g in gens:
            next(g, None)
    for l in range(2):
        u, dense, arr = prep[l]
        done = outs[l]
        upper = jnp.concatenate([d[0] for d in done], 0)
        upper = jnp.where(row <= col, upper, 0.0)
        panel = jnp.concatenate([d[1] for d in done], 0)
        inv = jnp.concatenate([d[2] for d in done], 0)
        f_ref[l] = upper.T
        p_ref[l] = panel
        shift = dot00_3(inv, panel).astype(BF)
        s_ref[l] = shift
        turned = jnp.dot(u[:, :128], shift, preferred_element_type=F32).astype(BF)
        d_ref[l] = jnp.concatenate([u[:, 128:], turned], 1)
        sk_ref[l] = dense[128:, 128:] - dot00_3(panel, panel)

def k0(bases, diag):
    sd = jax.ShapeDtypeStruct
    return pl.pallas_call(
        k0_body,
        in_specs=[pl.BlockSpec(memory_space=pltpu.HBM)] * 2,
        scratch_shapes=[
            pltpu.VMEM((2, 256, 256), BF),
            pltpu.VMEM((2, 256, 256), BF),
            pltpu.SemaphoreType.DMA((2,)),
        ],
        out_shape=(sd((2,128,128),F32), sd((2,128,128),F32), sd((2,128,128),F32), sd((2,128,128),BF), sd((2,256,256),BF)),
        compiler_params=pltpu.CompilerParams(vmem_limit_bytes=VMEM),
        cost_estimate=cost(6.5),
        name="leaf_elimination",
    )(bases, diag)


def slot_table(nbrs, table, device):
    for leaf in range(2):
        for w in range(WINDOW):
            table[leaf, w] = -1
        for n in range(SLOTS):
            j = nbrs[leaf, n]

            @pl.when(j >= 0)
            def _():
                table[leaf, j - 4 * (device // 2) + REACH] = n


def package_leaves(name, device):
    core = device % 2
    kind, k = name
    if kind == "own":
        return [16 + 2 * core + i for i in range(2)]
    if kind == "other":
        return [18 - 2 * core + i for i in range(2)]
    below = (core == 0) if kind == "near" else (core == 1)
    low, high = 4 * (4 - k), 4 * (4 + k)
    if k == 3:
        place = device // 2 % 4
        holder = core if kind == "near" else 1 - core
        end = jnp.where(holder == 0, place == 0, place == 3)
        turned = jnp.where((holder == 1) != end, 2, 0)
        return [jnp.where(holder == 0, high, low) + (i ^ turned) for i in range(4)]
    return [jnp.where(below, low + (i ^ 2), high + i) for i in range(4)]


def near_blocks_of(names, refs, h_ref, s_ref, table, device, put, group=8):
    work = []
    for leaf in range(2):
        index = 0
        for name, ref in zip(names, refs):
            for i, place in enumerate(package_leaves(name, device)):
                if not (name[0] == "own" and i == leaf):
                    work.append((leaf, index, place, ref, i))
                index += 1
    shifts = [s_ref[leaf].T for leaf in range(2)]
    for first in range(0, len(work), group):
        some = work[first : first + group]
        slots = [table[leaf, place] for leaf, _, place, _, _ in some]
        boths = [
            jnp.dot(h_ref[item[0], jnp.maximum(n, 0)], item[3][item[4]], preferred_element_type=F32)
            for item, n in zip(some, slots)
        ]
        rests = []
        for item, both in zip(some, boths):
            hi, lo = split(both[:RANK, :RANK])
            rests.append(jnp.dot(shifts[item[0]], jnp.concatenate([hi, lo], 1), preferred_element_type=F32))
        for (leaf, index, place, _, _), n, both, rest in zip(some, slots, boths, rests):
            block = both[RANK:, :RANK] - both[RANK:, RANK:] - rest[:, :RANK] - rest[:, RANK:]
            put(leaf, index, place, n, block)


def row_of(pnbrs, parent, goal, live, missing):
    q = jnp.int32(missing)
    for t in range(PNB):
        q = jnp.where((pnbrs[t, parent] == goal) & live, t, q)
    return q


def half_body(u_ref, a_ref, h_ref):
    for leaf in range(2):
        ut = u_ref[leaf].T
        for n in range(SLOTS):
            h_ref[leaf, n] = jnp.dot(ut, a_ref[leaf, n], preferred_element_type=F32).astype(BF)


def half_products(bases, near_blocks):
    vmem = pl.BlockSpec(memory_space=pltpu.VMEM)
    return pl.pallas_call(
        half_body,
        in_specs=[vmem, vmem],
        out_specs=vmem,
        out_shape=jax.ShapeDtypeStruct((2, SLOTS, 256, 256), BF),
        compiler_params=pltpu.CompilerParams(vmem_limit_bytes=VMEM),
        cost_estimate=cost(3.5),
        name="half_products",
    )(bases, near_blocks)


INNER = (("own", 0), ("other", 0), ("near", 1), ("far", 1), ("near", 4), ("far", 4))
LAST = (("near", 2), ("far", 2), ("near", 3), ("far", 3))


def inner_body(nbrs, s_ref, h_ref, sk_ref, *refs):
    pieces = refs[:6]
    rows_ref, ex_ref, part_ref, table = refs[6:]
    device = lax.axis_index("leaf")
    slot_table(nbrs, table, device)
    parent = device // 4
    rows_ref[...] = jnp.zeros_like(rows_ref)

    def put(leaf, index, place, n, block):
        j = place + 4 * (device // 2) - REACH
        part_ref[leaf, index] = block
        inside = (n >= 0) & (j // CHILDREN == parent)
        at = pl.multiple_of(jnp.where(inside, j % CHILDREN, CHILDREN) * RANK, RANK)
        rows_ref[leaf, :, pl.ds(at, RANK)] = block

    near_blocks_of(INNER, pieces, h_ref, s_ref, table, device, put)
    for leaf in range(2):
        mine = pl.multiple_of(((2 * device + leaf) % CHILDREN) * RANK, RANK)
        rows_ref[leaf, :, pl.ds(mine, RANK)] = sk_ref[leaf]
        part_ref[leaf, leaf] = sk_ref[leaf]
    place = device % 4
    for m in range(1, 4):
        at = pl.multiple_of((place ^ m) * 256, 256)
        block = jnp.concatenate([rows_ref[leaf, :, pl.ds(at, 256)] for leaf in range(2)], 0)
        ex_ref[m - 1] = block.T.astype(BF)


def inner(leaf_nbrs, shift, halves, skeleton, pieces):
    sd = jax.ShapeDtypeStruct
    vmem = pl.BlockSpec(memory_space=pltpu.VMEM)
    return pl.pallas_call(
        inner_body,
        in_specs=[pl.BlockSpec(memory_space=pltpu.SMEM)] + [vmem] * 9,
        out_specs=[vmem, vmem, vmem],
        scratch_shapes=[pltpu.SMEM((2, WINDOW), jnp.int32)],
        out_shape=(
            sd((2, RANK, (CHILDREN + 1) * RANK), F32),
            sd((3, 256, 256), BF),
            sd((2, 20, RANK, RANK), F32),
        ),
        compiler_params=pltpu.CompilerParams(vmem_limit_bytes=VMEM),
        cost_estimate=cost(0.01),
        name="inner_rows",
    )(leaf_nbrs, shift, halves, skeleton, *pieces)


def outer_body(nbrs, pnbrs, part_ref, out_ref, full, table, sems):
    device = lax.axis_index("leaf")
    slot_table(nbrs, table, device)
    parent = device // 4
    full[...] = jnp.zeros_like(full)
    copies = [
        pltpu.make_async_copy(full.at[leaf, pl.ds(0, PNB)], out_ref.at[leaf], sems.at[leaf]) for leaf in range(2)
    ]
    for leaf in range(2):
        index = 0
        for name in INNER:
            for i, place in enumerate(package_leaves(name, device)):
                mine = name[0] == "own" and i == leaf
                live = True if mine else table[leaf, place] >= 0
                j = place + 4 * (device // 2) - REACH
                q = row_of(pnbrs, parent, j // CHILDREN, live, PNB)
                at = pl.multiple_of((j % CHILDREN) * RANK, RANK)
                full[leaf, q, :, pl.ds(at, RANK)] = part_ref[leaf, index]
                index += 1
        copies[leaf].start()
    for c in copies:
        c.wait()


def outer(leaf_nbrs, parent_nbrs, part):
    return pl.pallas_call(
        outer_body,
        in_specs=[pl.BlockSpec(memory_space=pltpu.SMEM)] * 2 + [pl.BlockSpec(memory_space=pltpu.VMEM)],
        out_specs=pl.BlockSpec(memory_space=pl.ANY),
        scratch_shapes=[
            pltpu.VMEM((2, PNB + 1, RANK, CHILDREN * RANK), F32),
            pltpu.SMEM((2, WINDOW), jnp.int32),
            pltpu.SemaphoreType.DMA((2,)),
        ],
        out_shape=jax.ShapeDtypeStruct((2, PNB, RANK, CHILDREN * RANK), F32),
        compiler_params=pltpu.CompilerParams(vmem_limit_bytes=VMEM),
        cost_estimate=cost(0.01),
        name="outer_rows",
    )(leaf_nbrs, parent_nbrs, part)


def last_body(nbrs, pnbrs, s_ref, h_ref, rows_ref, r1_ref, r2_ref, r3_ref, *refs):
    pieces = refs[:4]
    _, out_ref, block_ref, part, table, sems = refs[4:]
    device = lax.axis_index("leaf")
    slot_table(nbrs, table, device)
    parent = device // 4
    copies = []

    def put(leaf, index, place, n, block):
        j = place + 4 * (device // 2) - REACH
        part[leaf, index] = block
        q = row_of(pnbrs, parent, j // CHILDREN, n >= 0, -1)
        at = pl.multiple_of((j % CHILDREN) * RANK, RANK)
        copy = pltpu.make_async_copy(
            part.at[leaf, index],
            out_ref.at[leaf, jnp.maximum(q, 0), :, pl.ds(at, RANK)],
            sems.at[leaf, index],
        )
        copies.append((q, copy))

        @pl.when(q >= 0)
        def _():
            copy.start()

    near_blocks_of(LAST, pieces, h_ref, s_ref, table, device, put)
    place = device % 4
    for m, ref in enumerate((None, r1_ref, r2_ref, r3_ref)):
        at = pl.multiple_of((place ^ m) * 256, 256)
        own = jnp.concatenate([rows_ref[leaf, :, pl.ds(at, 256)] for leaf in range(2)], 0)
        turned = own.T if m == 0 else ref[...].astype(F32)
        block_ref[:, pl.ds(at, 256)] = 0.5 * (own + turned)
    for q, copy in copies:

        @pl.when(q >= 0)
        def _():
            copy.wait()


def last(leaf_nbrs, parent_nbrs, shift, halves, rows, received, pieces, merged):
    sd = jax.ShapeDtypeStruct
    vmem = pl.BlockSpec(memory_space=pltpu.VMEM)
    hbm = pl.BlockSpec(memory_space=pl.ANY)
    return pl.pallas_call(
        last_body,
        in_specs=[pl.BlockSpec(memory_space=pltpu.SMEM)] * 2 + [vmem] * 10 + [hbm],
        out_specs=[hbm, vmem],
        scratch_shapes=[
            pltpu.VMEM((2, 16, RANK, RANK), F32),
            pltpu.SMEM((2, WINDOW), jnp.int32),
            pltpu.SemaphoreType.DMA((2, 16)),
        ],
        out_shape=(sd((2, PNB, RANK, CHILDREN * RANK), F32), sd((256, CHILDREN * RANK), F32)),
        input_output_aliases={12: 0},
        compiler_params=pltpu.CompilerParams(vmem_limit_bytes=VMEM),
        cost_estimate=cost(0.01),
        name="last_rows",
    )(leaf_nbrs, parent_nbrs, shift, halves, rows, *received, *pieces, merged)


def ring_body(own_ref, far_ref, out_ref, sem):
    device = lax.axis_index("leaf")
    place = device // 2 % 4
    end = jnp.where(device % 2 == 0, place == 0, place == 3)

    @pl.when(end)
    def _():
        copy = pltpu.make_async_copy(own_ref, out_ref, sem)
        copy.start()
        copy.wait()

    @pl.when(jnp.logical_not(end))
    def _():
        copy = pltpu.make_async_copy(far_ref, out_ref, sem)
        copy.start()
        copy.wait()


def ring_package(own, far):
    return pl.pallas_call(
        ring_body,
        in_specs=[pl.BlockSpec(memory_space=pl.ANY)] * 2,
        out_specs=pl.BlockSpec(memory_space=pl.ANY),
        scratch_shapes=[pltpu.SemaphoreType.DMA],
        out_shape=jax.ShapeDtypeStruct(own.shape, own.dtype),
        compiler_params=pltpu.CompilerParams(vmem_limit_bytes=1024 * 1024),
        cost_estimate=cost(0.01),
        name="ring_package",
    )(own, far)


def swap(value, mask):
    pairs = [(source, source ^ mask) for source in range(lax.axis_size("leaf"))]
    return lax.ppermute(value, "leaf", pairs)


def across(value, apart):
    count = lax.axis_size("leaf")
    pairs = count // 2
    matched = [(2 * c + 1, 2 * (c + apart)) for c in range(pairs - apart)]
    low = [2 * c for c in range(min(apart, pairs))]
    high = [2 * c + 1 for c in range(max(pairs - apart, 0), pairs)]
    while len(low) > 1:
        matched += [(low.pop(), low.pop()), (high.pop(), high.pop())]
    if low:
        matched.append((low.pop(), high.pop()))
    return lax.ppermute(value, "leaf", matched + [(b, a) for a, b in matched])


def around(value):
    matched = []
    for lower in range(1, lax.axis_size("leaf"), 2):
        ring, place = divmod(lower // 2, 4)
        matched.append((lower, 2 * (4 * ring + (place + 1) % 4)))
    return lax.ppermute(value, "leaf", matched + [(b, a) for a, b in matched])


def local(near_blocks, diag_blocks, bases, leaf_nbrs, parent_nbrs):
    barrier = lax.optimization_barrier
    leaf_factor, leaf_panel, skeleton, shift, own = k0(
        pltpu.with_memory_space_constraint(bases, pltpu.HBM),
        pltpu.with_memory_space_constraint(diag_blocks, pltpu.HBM),
    )
    other = swap(own, 1)
    both = jnp.concatenate([own, other])
    first, fourth = across(both, 1), across(both, 4)
    halves = half_products(barrier((bases, other))[0], near_blocks)
    halves, first, fourth = barrier((halves, first, fourth))
    first_other, fourth_other = swap(first, 1), swap(fourth, 1)
    second = across(first_other, 1)
    third = around(ring_package(both, fourth))
    rows, exchange, part = inner(
        leaf_nbrs, shift, halves, skeleton, (own, other, first, first_other, fourth, fourth_other)
    )
    received = [swap(exchange[m - 1], m) for m in range(1, 4)]
    merged = outer(leaf_nbrs, parent_nbrs.T, part)
    merged, second, third, *received = barrier((merged, second, third, *received))
    merged, parent_block = last(
        leaf_nbrs, parent_nbrs.T, shift, halves, rows, received,
        (second, swap(second, 1), third, swap(third, 1)), merged,
    )
    return (leaf_factor, leaf_panel, merged, parent_block)


def solution(mesh):
    in_specs = (
        P("leaf", None, None, None),
        P("leaf", None, None),
        P("leaf", None, None),
        P("leaf", None),
        P(),
    )
    out_specs = (
        P("leaf", None, None),
        P("leaf", None, None),
        P("leaf", None, None, None),
        P("leaf", None),
    )
    return jax.shard_map(local, mesh=mesh, in_specs=in_specs, out_specs=out_specs, check_vma=False)
```

```python
import jax
import jax.numpy as jnp
from jax import lax
from jax.experimental import pallas as pl
from jax.experimental.pallas import tpu as pltpu
from jax.sharding import PartitionSpec as P

RANK = 128
REACH = 16
CHILDREN = 8
SLOTS = 26
PNB = 5
REACH_CHIPS = 4
WINDOW = 36
GROUP = 6 + 7
RATE = 1.1e15
VMEM = 24 * 1024 * 1024


F32 = jnp.float32
BF = jnp.bfloat16

def split(x):
    hi = x.astype(BF)
    lo = (x - hi.astype(F32)).astype(BF)
    return hi, lo

def dot00(a, b):
    return lax.dot_general(a, b, (((0,), (0,)), ((), ())), preferred_element_type=F32)

def dot00_3(a, b):
    ah, al = split(a); bh, bl = split(b)
    return dot00(jnp.concatenate([ah, ah, al], 0), jnp.concatenate([bh, bl, bh], 0))

def bc(x):
    return jnp.broadcast_to(x, (8, 128))

def eliminate(blocks, out):
    sub = lax.broadcasted_iota(jnp.int32, (8, 128), 0)
    count = len(blocks)
    done = []
    for k in range(count):
        yield
        parts = blocks[k]
        left = parts[0]
        cols = [bc(left[:, 8*k+j:8*k+j+1]) for j in range(8)]
        s = [[bc(cols[j][i:i+1, :]) for j in range(i+1)] for i in range(8)]
        r = [None]*8
        L = [[None]*8 for _ in range(8)]
        for j in range(8):
            r[j] = lax.rsqrt(s[j][j])
            for i in range(j+1, 8):
                L[i][j] = s[i][j]*r[j]
            for i in range(j+1, 8):
                for m in range(j+1, i+1):
                    s[i][m] = s[i][m] - L[i][j]*L[m][j]
        rows = []
        for j in range(8):
            row = []
            for q, part in enumerate(parts):
                x = bc(part[j:j+1, :])
                for m in range(j):
                    x = x - L[j][m]*rows[m][q]
                row.append(x*r[j])
            rows.append(row)
        packed = []
        for q in range(len(parts)):
            x = rows[0][q]
            for j in range(1, 8):
                x = jnp.where(sub == j, rows[j][q], x)
            packed.append(x)
        done.append(packed)
        if k + 1 < count:
            nxt = blocks[k+1]
            cb = [bc(nxt[0][:, 8*k+j:8*k+j+1]) for j in range(8)]
            lc = []
            new = list(nxt)
            for j in range(8):
                x = cb[j]
                for m in range(j):
                    x = x - lc[m]*L[j][m]
                x = x*r[j]
                lc.append(x)
                new = [new[q] - x*rows[j][q] for q in range(len(new))]
            blocks[k+1] = new
        if k + 2 < count:
            wide = jnp.concatenate(packed, 1)
            upd = dot00_3(packed[0], wide)
            for ib in range(k+2, count):
                blocks[ib] = [blocks[ib][q] - upd[8*ib:8*ib+8, 128*q:128*q+128] for q in range(len(packed))]
    out.extend(done)

def cost(microseconds):
    return pl.CostEstimate(flops=int(microseconds * 1e-6 * RATE), bytes_accessed=0, transcendentals=0)


def k0_body(u_hbm, a_hbm, f_ref, p_ref, sk_ref, s_ref, d_ref, u_ref, a_ref, sems):
    loads = [
        pltpu.make_async_copy(u_hbm, u_ref, sems.at[0]),
        pltpu.make_async_copy(a_hbm, a_ref, sems.at[1]),
    ]
    for load in loads:
        load.start()
    for load in loads:
        load.wait()
    row = lax.broadcasted_iota(jnp.int32, (128, 128), 0)
    col = lax.broadcasted_iota(jnp.int32, (128, 128), 1)
    eye = jnp.where(row == col, 1.0, 0.0).astype(F32)
    outs = []; gens = []
    prep = []
    for l in range(2):
        u = u_ref[l]
        half = dot00(u, a_ref[l]).astype(BF)
        dense = jnp.dot(half, u, preferred_element_type=F32)
        arr = dense[:128, :128]
        arr = 0.5*(arr + arr.T)
        prep.append((u, dense, arr))
    for l in range(2):
        u, dense, arr = prep[l]
        rs = dense[:128, 128:]
        blocks = [[arr[8*i:8*i+8], rs[8*i:8*i+8], eye[8*i:8*i+8]] for i in range(16)]
        outs.append([])
        gens.append(eliminate(blocks, outs[-1]))
    for _ in range(17):
        for g in gens:
            next(g, None)
    for l in range(2):
        u, dense, arr = prep[l]
        done = outs[l]
        upper = jnp.concatenate([d[0] for d in done], 0)
        upper = jnp.where(row <= col, upper, 0.0)
        panel = jnp.concatenate([d[1] for d in done], 0)
        inv = jnp.concatenate([d[2] for d in done], 0)
        f_ref[l] = upper.T
        p_ref[l] = panel
        shift = dot00_3(inv, panel).astype(BF)
        s_ref[l] = shift
        turned = jnp.dot(u[:, :128], shift, preferred_element_type=F32).astype(BF)
        d_ref[l] = jnp.concatenate([u[:, 128:], turned], 1)
        sk_ref[l] = dense[128:, 128:] - dot00_3(panel, panel)

def k0(bases, diag):
    sd = jax.ShapeDtypeStruct
    return pl.pallas_call(
        k0_body,
        in_specs=[pl.BlockSpec(memory_space=pltpu.HBM)] * 2,
        scratch_shapes=[
            pltpu.VMEM((2, 256, 256), BF),
            pltpu.VMEM((2, 256, 256), BF),
            pltpu.SemaphoreType.DMA((2,)),
        ],
        out_shape=(sd((2,128,128),F32), sd((2,128,128),F32), sd((2,128,128),F32), sd((2,128,128),BF), sd((2,256,256),BF)),
        compiler_params=pltpu.CompilerParams(vmem_limit_bytes=VMEM),
        cost_estimate=cost(6.5),
        name="leaf_elimination",
    )(bases, diag)


def slot_table(nbrs, table, device):
    for leaf in range(2):
        for w in range(WINDOW):
            table[leaf, w] = -1
        for n in range(SLOTS):
            j = nbrs[leaf, n]

            @pl.when(j >= 0)
            def _():
                table[leaf, j - 4 * (device // 2) + REACH] = n


def package_leaves(name, device):
    core = device % 2
    kind, k = name
    if kind == "own":
        return [16 + 2 * core + i for i in range(2)]
    if kind == "other":
        return [18 - 2 * core + i for i in range(2)]
    below = (core == 0) if kind == "near" else (core == 1)
    low, high = 4 * (4 - k), 4 * (4 + k)
    if k == 3:
        place = device // 2 % 4
        holder = core if kind == "near" else 1 - core
        end = jnp.where(holder == 0, place == 0, place == 3)
        turned = jnp.where((holder == 1) != end, 2, 0)
        return [jnp.where(holder == 0, high, low) + (i ^ turned) for i in range(4)]
    return [jnp.where(below, low + (i ^ 2), high + i) for i in range(4)]


def near_blocks_of(names, refs, h_ref, s_ref, table, device, put, group=8):
    work = []
    for leaf in range(2):
        index = 0
        for name, ref in zip(names, refs):
            for i, place in enumerate(package_leaves(name, device)):
                if not (name[0] == "own" and i == leaf):
                    work.append((leaf, index, place, ref, i))
                index += 1
    shifts = [s_ref[leaf].T for leaf in range(2)]
    for first in range(0, len(work), group):
        some = work[first : first + group]
        slots = [table[leaf, place] for leaf, _, place, _, _ in some]
        boths = [
            jnp.dot(h_ref[item[0], jnp.maximum(n, 0)], item[3][item[4]], preferred_element_type=F32)
            for item, n in zip(some, slots)
        ]
        rests = []
        for item, both in zip(some, boths):
            hi, lo = split(both[:RANK, :RANK])
            rests.append(jnp.dot(shifts[item[0]], jnp.concatenate([hi, lo], 1), preferred_element_type=F32))
        for (leaf, index, place, _, _), n, both, rest in zip(some, slots, boths, rests):
            block = both[RANK:, :RANK] - both[RANK:, RANK:] - rest[:, :RANK] - rest[:, RANK:]
            put(leaf, index, place, n, block)


def row_of(pnbrs, parent, goal, live, missing):
    q = jnp.int32(missing)
    for t in range(PNB):
        q = jnp.where((pnbrs[t, parent] == goal) & live, t, q)
    return q


def half_body(u_ref, a_ref, h_ref):
    for leaf in range(2):
        ut = u_ref[leaf].T
        for n in range(SLOTS):
            h_ref[leaf, n] = jnp.dot(ut, a_ref[leaf, n], preferred_element_type=F32).astype(BF)


def half_products(bases, near_blocks):
    vmem = pl.BlockSpec(memory_space=pltpu.VMEM)
    return pl.pallas_call(
        half_body,
        in_specs=[vmem, vmem],
        out_specs=vmem,
        out_shape=jax.ShapeDtypeStruct((2, SLOTS, 256, 256), BF),
        compiler_params=pltpu.CompilerParams(vmem_limit_bytes=VMEM),
        cost_estimate=cost(3.5),
        name="half_products",
    )(bases, near_blocks)


INNER = (("own", 0), ("other", 0), ("near", 1), ("far", 1), ("near", 4), ("far", 4))
LAST = (("near", 2), ("far", 2), ("near", 3), ("far", 3))


def inner_body(nbrs, s_ref, h_ref, sk_ref, *refs):
    pieces = refs[:6]
    rows_ref, ex_ref, part_ref, table = refs[6:]
    device = lax.axis_index("leaf")
    slot_table(nbrs, table, device)
    parent = device // 4
    rows_ref[...] = jnp.zeros_like(rows_ref)

    def put(leaf, index, place, n, block):
        j = place + 4 * (device // 2) - REACH
        part_ref[leaf, index] = block
        inside = (n >= 0) & (j // CHILDREN == parent)
        at = pl.multiple_of(jnp.where(inside, j % CHILDREN, CHILDREN) * RANK, RANK)
        rows_ref[leaf, :, pl.ds(at, RANK)] = block

    near_blocks_of(INNER, pieces, h_ref, s_ref, table, device, put)
    for leaf in range(2):
        mine = pl.multiple_of(((2 * device + leaf) % CHILDREN) * RANK, RANK)
        rows_ref[leaf, :, pl.ds(mine, RANK)] = sk_ref[leaf]
        part_ref[leaf, leaf] = sk_ref[leaf]
    place = device % 4
    for m in range(1, 4):
        at = pl.multiple_of((place ^ m) * 256, 256)
        block = jnp.concatenate([rows_ref[leaf, :, pl.ds(at, 256)] for leaf in range(2)], 0)
        ex_ref[m - 1] = block.T.astype(BF)


def inner(leaf_nbrs, shift, halves, skeleton, pieces):
    sd = jax.ShapeDtypeStruct
    vmem = pl.BlockSpec(memory_space=pltpu.VMEM)
    return pl.pallas_call(
        inner_body,
        in_specs=[pl.BlockSpec(memory_space=pltpu.SMEM)] + [vmem] * 9,
        out_specs=[vmem, vmem, vmem],
        scratch_shapes=[pltpu.SMEM((2, WINDOW), jnp.int32)],
        out_shape=(
            sd((2, RANK, (CHILDREN + 1) * RANK), F32),
            sd((3, 256, 256), BF),
            sd((2, 20, RANK, RANK), F32),
        ),
        compiler_params=pltpu.CompilerParams(vmem_limit_bytes=VMEM),
        cost_estimate=cost(0.01),
        name="inner_rows",
    )(leaf_nbrs, shift, halves, skeleton, *pieces)


def outer_body(nbrs, pnbrs, part_ref, out_ref, full, table, sems):
    device = lax.axis_index("leaf")
    slot_table(nbrs, table, device)
    parent = device // 4
    full[...] = jnp.zeros_like(full)
    copies = [
        pltpu.make_async_copy(full.at[leaf, pl.ds(0, PNB)], out_ref.at[leaf], sems.at[leaf]) for leaf in range(2)
    ]
    for leaf in range(2):
        index = 0
        for name in INNER:
            for i, place in enumerate(package_leaves(name, device)):
                mine = name[0] == "own" and i == leaf
                live = True if mine else table[leaf, place] >= 0
                j = place + 4 * (device // 2) - REACH
                q = row_of(pnbrs, parent, j // CHILDREN, live, PNB)
                at = pl.multiple_of((j % CHILDREN) * RANK, RANK)
                full[leaf, q, :, pl.ds(at, RANK)] = part_ref[leaf, index]
                index += 1
        copies[leaf].start()
    for c in copies:
        c.wait()


def outer(leaf_nbrs, parent_nbrs, part):
    return pl.pallas_call(
        outer_body,
        in_specs=[pl.BlockSpec(memory_space=pltpu.SMEM)] * 2 + [pl.BlockSpec(memory_space=pltpu.VMEM)],
        out_specs=pl.BlockSpec(memory_space=pl.ANY),
        scratch_shapes=[
            pltpu.VMEM((2, PNB + 1, RANK, CHILDREN * RANK), F32),
            pltpu.SMEM((2, WINDOW), jnp.int32),
            pltpu.SemaphoreType.DMA((2,)),
        ],
        out_shape=jax.ShapeDtypeStruct((2, PNB, RANK, CHILDREN * RANK), F32),
        compiler_params=pltpu.CompilerParams(vmem_limit_bytes=VMEM),
        cost_estimate=cost(0.01),
        name="outer_rows",
    )(leaf_nbrs, parent_nbrs, part)


def last_body(nbrs, pnbrs, s_ref, h_ref, rows_ref, r1_ref, r2_ref, r3_ref, *refs):
    pieces = refs[:4]
    _, out_ref, block_ref, part, table, sems = refs[4:]
    device = lax.axis_index("leaf")
    slot_table(nbrs, table, device)
    parent = device // 4
    copies = []

    def put(leaf, index, place, n, block):
        j = place + 4 * (device // 2) - REACH
        part[leaf, index] = block
        q = row_of(pnbrs, parent, j // CHILDREN, n >= 0, -1)
        at = pl.multiple_of((j % CHILDREN) * RANK, RANK)
        copy = pltpu.make_async_copy(
            part.at[leaf, index],
            out_ref.at[leaf, jnp.maximum(q, 0), :, pl.ds(at, RANK)],
            sems.at[leaf, index],
        )
        copies.append((q, copy))

        @pl.when(q >= 0)
        def _():
            copy.start()

    near_blocks_of(LAST, pieces, h_ref, s_ref, table, device, put)
    place = device % 4
    for m, ref in enumerate((None, r1_ref, r2_ref, r3_ref)):
        at = pl.multiple_of((place ^ m) * 256, 256)
        own = jnp.concatenate([rows_ref[leaf, :, pl.ds(at, 256)] for leaf in range(2)], 0)
        turned = own.T if m == 0 else ref[...].astype(F32)
        block_ref[:, pl.ds(at, 256)] = 0.5 * (own + turned)
    for q, copy in copies:

        @pl.when(q >= 0)
        def _():
            copy.wait()


def last(leaf_nbrs, parent_nbrs, shift, halves, rows, received, pieces, merged):
    sd = jax.ShapeDtypeStruct
    vmem = pl.BlockSpec(memory_space=pltpu.VMEM)
    hbm = pl.BlockSpec(memory_space=pl.ANY)
    return pl.pallas_call(
        last_body,
        in_specs=[pl.BlockSpec(memory_space=pltpu.SMEM)] * 2 + [vmem] * 10 + [hbm],
        out_specs=[hbm, vmem],
        scratch_shapes=[
            pltpu.VMEM((2, 16, RANK, RANK), F32),
            pltpu.SMEM((2, WINDOW), jnp.int32),
            pltpu.SemaphoreType.DMA((2, 16)),
        ],
        out_shape=(sd((2, PNB, RANK, CHILDREN * RANK), F32), sd((256, CHILDREN * RANK), F32)),
        input_output_aliases={12: 0},
        compiler_params=pltpu.CompilerParams(vmem_limit_bytes=VMEM),
        cost_estimate=cost(0.01),
        name="last_rows",
    )(leaf_nbrs, parent_nbrs, shift, halves, rows, *received, *pieces, merged)


def ring_body(own_ref, far_ref, out_ref, sem):
    device = lax.axis_index("leaf")
    place = device // 2 % 4
    end = jnp.where(device % 2 == 0, place == 0, place == 3)

    @pl.when(end)
    def _():
        copy = pltpu.make_async_copy(own_ref, out_ref, sem)
        copy.start()
        copy.wait()

    @pl.when(jnp.logical_not(end))
    def _():
        copy = pltpu.make_async_copy(far_ref, out_ref, sem)
        copy.start()
        copy.wait()


def ring_package(own, far):
    return pl.pallas_call(
        ring_body,
        in_specs=[pl.BlockSpec(memory_space=pl.ANY)] * 2,
        out_specs=pl.BlockSpec(memory_space=pl.ANY),
        scratch_shapes=[pltpu.SemaphoreType.DMA],
        out_shape=jax.ShapeDtypeStruct(own.shape, own.dtype),
        compiler_params=pltpu.CompilerParams(vmem_limit_bytes=1024 * 1024),
        cost_estimate=cost(0.01),
        name="ring_package",
    )(own, far)


def swap(value, mask):
    pairs = [(source, source ^ mask) for source in range(lax.axis_size("leaf"))]
    return lax.ppermute(value, "leaf", pairs)


def across(value, apart):
    count = lax.axis_size("leaf")
    pairs = count // 2
    matched = [(2 * c + 1, 2 * (c + apart)) for c in range(pairs - apart)]
    low = [2 * c for c in range(min(apart, pairs))]
    high = [2 * c + 1 for c in range(max(pairs - apart, 0), pairs)]
    while len(low) > 1:
        matched += [(low.pop(), low.pop()), (high.pop(), high.pop())]
    if low:
        matched.append((low.pop(), high.pop()))
    return lax.ppermute(value, "leaf", matched + [(b, a) for a, b in matched])


def around(value):
    matched = []
    for lower in range(1, lax.axis_size("leaf"), 2):
        ring, place = divmod(lower // 2, 4)
        matched.append((lower, 2 * (4 * ring + (place + 1) % 4)))
    return lax.ppermute(value, "leaf", matched + [(b, a) for a, b in matched])


def local(near_blocks, diag_blocks, bases, leaf_nbrs, parent_nbrs):
    barrier = lax.optimization_barrier
    leaf_factor, leaf_panel, skeleton, shift, own = k0(
        pltpu.with_memory_space_constraint(bases, pltpu.HBM),
        pltpu.with_memory_space_constraint(diag_blocks, pltpu.HBM),
    )
    other = swap(own, 1)
    both = jnp.concatenate([own, other])
    first, fourth = across(both, 1), across(both, 4)
    halves = half_products(barrier((bases, other))[0], near_blocks)
    halves, first, fourth = barrier((halves, first, fourth))
    first_other, fourth_other = swap(first, 1), swap(fourth, 1)
    second = across(first_other, 1)
    third = around(ring_package(both, fourth))
    rows, exchange, part = inner(
        leaf_nbrs, shift, halves, skeleton, (own, other, first, first_other, fourth, fourth_other)
    )
    received = [swap(exchange[m - 1], m) for m in range(1, 4)]
    merged = outer(leaf_nbrs, parent_nbrs.T, part)
    merged, third = barrier((merged, third))
    third_other = swap(third, 1)
    merged, second, *received = barrier((merged, second, *received))
    merged, parent_block = last(
        leaf_nbrs, parent_nbrs.T, shift, halves, rows, received,
        (second, swap(second, 1), third, third_other), merged,
    )
    return (leaf_factor, leaf_panel, merged, parent_block)


def solution(mesh):
    in_specs = (
        P("leaf", None, None, None),
        P("leaf", None, None),
        P("leaf", None, None),
        P("leaf", None),
        P(),
    )
    out_specs = (
        P("leaf", None, None),
        P("leaf", None, None),
        P("leaf", None, None, None),
        P("leaf", None),
    )
    return jax.shard_map(local, mesh=mesh, in_specs=in_specs, out_specs=out_specs, check_vma=False)
```
